256 devices in a mesh: param: 32 (over z, y_lo, core), sensor: 8 (over y_hi, x).
Axes of the slice: x: 4, y: 4 (y_hi: 2, y_lo: 2; y = y_hi * 2 + y_lo), z: 8, core: 2. Of those that a mesh axis runs over, the one named last changes fastest.
Arguments:
- kernel_spec: float32 [2, 96, 8, 512, 421], P(None, 'param', None, 'sensor'), may hold values from -1 to 1, as said below
- observed: float32 [512, 420], P('sensor'), may hold values from -6 to 6
- initial: float32 [96, 8, 420], P('param'), may hold values from 0 to 1, as said below
Outputs:
- sources: float32 [96, 8, 420], P('param')
- residual: float32 [512, 420], P('sensor')
The draws below stay inside these ranges and needn't reach their ends.
Inputs may be any that keep to these rules, and one draw needn't show every extreme that they name: `kernel_spec`: real and imaginary parts of the transformed Green's function of each source point and sensor. `initial`: nonnegative starting source histories.
All inputs are finite; a program needn't handle non-finite values.
Results may differ from the reference program's by a relative error of at most 0.0001.
Values sent between devices are 32-bit elements; how exact they have to be, the bound alone decides.
No kernel may reach another device: no remote copies, remote signals or barrier semaphores. Data moves between devices by JAX's collectives and lax.ppermute only.
A program may use at most 64 MiB of HBM per device.

```python
import math
import jax
import jax.numpy as jnp
from jax import lax

NT = 420
NF = 421
SENSORS = 512
DIP = 8
STRIKE = 96
ITERS = 2


def draw_kernel_spec(key, part):
    keys = jax.random.split(jax.random.fold_in(key, 17), 4)
    shape = (STRIKE, DIP, SENSORS, 1)
    base = 1.0 + 0.5 * jax.random.normal(keys[0], shape, jnp.float32)
    base = jnp.clip(base, -0.5, 2.0)
    column = 1.0 + 2.0 * jnp.arange(STRIKE, dtype=jnp.float32).reshape(STRIKE, 1, 1, 1) / STRIKE
    amplitude = base * column * (2.0 / (STRIKE * DIP))
    quantum = max(1, NT // 35)
    first_steps = jax.random.randint(keys[1], shape, 1, 6 * NT // (10 * quantum) + 1)
    later_steps = jax.random.randint(keys[3], shape, 1, 3 * NT // (10 * quantum) + 1)
    delay = (quantum * first_steps).astype(jnp.float32)
    later = (quantum * (first_steps + later_steps)).astype(jnp.float32)
    spread = jax.random.uniform(keys[2], shape, jnp.float32, 0.1, 0.4)
    omega = jnp.arange(NF, dtype=jnp.float32) * (math.pi / NT)
    envelope = amplitude * jnp.exp(-0.5 * (omega * spread) ** 2)
    real_part = envelope * (jnp.cos(omega * delay) - 0.4 * jnp.cos(omega * later))
    imag_part = -envelope * (jnp.sin(omega * delay) - 0.4 * jnp.sin(omega * later))
    return jnp.stack([real_part, imag_part]).astype(jnp.float32)


def draw_initial(key, part):
    keys = jax.random.split(jax.random.fold_in(key, 29), 1)
    shape = (STRIKE, DIP, NT)
    times = jnp.arange(NT, dtype=jnp.float32).reshape(1, 1, NT)
    level = jax.random.uniform(keys[0], shape, jnp.float32, 0.0, 1.0)
    wave = 0.35 * jnp.cos(0.5 * math.pi * times) + 0.25 * jnp.cos(2.0 * math.pi / 3.0 * times)
    return jnp.clip(level + wave, 0.0, 1.0).astype(jnp.float32)


def block_scale(own_key, dims, cuts, low, high):
    def one(dim, parts):
        draws = jax.random.uniform(jax.random.fold_in(jax.random.fold_in(own_key, 6), dim), (parts,), jnp.float32, low / len(cuts), high / len(cuts))
        return jnp.repeat(jnp.exp(draws), dims[dim] // parts).reshape((-1,) + (1,) * (len(dims) - dim - 1))

    gain = one(*cuts[0])
    for cut in cuts[1:]:
        gain = gain * one(*cut)
    return gain


def centred(own_key, extent, scale, reach, cuts=(), kind=jnp.bfloat16):
    values = scale * jax.random.normal(own_key, extent, jnp.float32)
    if cuts:
        values = values * block_scale(own_key, extent, cuts, -0.22, 0.18)
    return jnp.clip(values, -reach, reach).astype(kind)


def setup_inputs(seed: int = 0) -> dict:
    splits = jax.random.split(jax.random.key(seed), 4)
    kernel_spec = draw_kernel_spec(jax.random.fold_in(splits[3], 71), 0)
    observed = centred(splits[1], (SENSORS, NT), 1.0, 6.0, ((0, 8),), jnp.float32)
    initial = draw_initial(jax.random.fold_in(splits[3], 71), 0)
    return dict(kernel_spec=kernel_spec, observed=observed, initial=initial)


HIGH = lax.Precision.HIGHEST
LAMBDA_REG = 0.5
TINY_TERM = 1e-6


def spectrum(series):
    trans = jnp.fft.rfft(series, n=2 * NT, axis=-1)
    return jnp.real(trans), jnp.imag(trans)


def series_of(real_part, imag_part):
    return jnp.fft.irfft(real_part + 1j * imag_part, n=2 * NT, axis=-1)[..., :NT]


def forward(kernel_spec, field):
    real_src, imag_src = spectrum(field)
    real_out = jnp.einsum("cdsf,cdf->sf", kernel_spec[0], real_src, precision=HIGH) - jnp.einsum("cdsf,cdf->sf", kernel_spec[1], imag_src, precision=HIGH)
    imag_out = jnp.einsum("cdsf,cdf->sf", kernel_spec[0], imag_src, precision=HIGH) + jnp.einsum("cdsf,cdf->sf", kernel_spec[1], real_src, precision=HIGH)
    return series_of(real_out, imag_out)


def adjoint(kernel_spec, misfit):
    real_res, imag_res = spectrum(misfit)
    real_out = jnp.einsum("cdsf,sf->cdf", kernel_spec[0], real_res, precision=HIGH) + jnp.einsum("cdsf,sf->cdf", kernel_spec[1], imag_res, precision=HIGH)
    imag_out = jnp.einsum("cdsf,sf->cdf", kernel_spec[0], imag_res, precision=HIGH) - jnp.einsum("cdsf,sf->cdf", kernel_spec[1], real_res, precision=HIGH)
    return series_of(real_out, imag_out)


def smoothing(field):
    padded = jnp.pad(field, ((1, 1), (1, 1), (0, 0)))
    return 4.0 * field - padded[2:, 1:-1] - padded[:-2, 1:-1] - padded[1:-1, 2:] - padded[1:-1, :-2]


def reference(kernel_spec, observed, initial):
    sources = initial
    residual = observed
    for iteration in range(ITERS):
        residual = forward(kernel_spec, sources) - observed
        gradient = adjoint(kernel_spec, residual) + LAMBDA_REG * smoothing(sources)
        image = forward(kernel_spec, gradient)
        grad_sq = jnp.sum(gradient * gradient)
        image_sq = jnp.sum(image * image)
        alpha = grad_sq / (image_sq + 8.0 * LAMBDA_REG * grad_sq + TINY_TERM)
        sources = jnp.maximum(sources - alpha * gradient, 0.0)
    return sources, residual
```

```python
import functools
import math

import jax
import jax.numpy as jnp
import numpy as np
from jax import lax
from jax.experimental import pallas as pl
from jax.experimental.pallas import tpu as pltpu
from jax.sharding import PartitionSpec as P

ITERS = 2
LAMBDA_REG = 0.5
TINY_TERM = 1e-06
LANES = 128
ROWS = 8
F32 = jnp.float32
BF16 = jnp.bfloat16
VMEM_LIMIT = 20 * 1024 * 1024


def dft_table(steps, freqs, pad):
    index = np.arange(pad, dtype=np.int64)
    phase = (index[:, None] * index[None, :]) % (2 * steps)
    angle = phase * (math.pi / steps)
    inside = (index[:, None] < freqs) & (index[None, :] < freqs)
    whole = np.concatenate(
        [np.where(inside, np.cos(angle), 0.0), np.where(inside, -np.sin(angle), 0.0)], axis=1
    )
    high = whole.astype(np.float32).astype(BF16)
    low = (whole - high.astype(np.float64)).astype(np.float32).astype(BF16)
    return high, low


def split(x):
    high = x.astype(BF16)
    low = (x - high.astype(F32)).astype(BF16)
    return high, low


def product(x, high_ref, low_ref, columns):
    xh, xl = split(x)
    high = high_ref[:, columns]
    dot = functools.partial(jnp.dot, preferred_element_type=F32)
    return dot(xh, high) + dot(xl, high) + dot(xh, low_ref[:, columns])


def to_series(real_part, imag_part, high_ref, low_ref, steps):
    pad = real_part.shape[1]
    column = lax.broadcasted_iota(jnp.int32, (1, pad), 1)
    weight = jnp.where((column == 0) | (column == steps), 1.0, 2.0) / (2.0 * steps)
    out = product(real_part * weight, high_ref, low_ref, slice(0, pad))
    out += product(imag_part * weight, high_ref, low_ref, slice(pad, 2 * pad))
    return jnp.where(column < steps, out, 0.0)


def lane_blocks(freqs):
    return [(start, min(LANES, freqs - start)) for start in range(0, freqs, LANES)]


def forward_map(field, k_ref, high_ref, low_ref, xs_ref, ys_ref, out_ref, steps):
    _, cols, dips, sensors, freqs = k_ref.shape
    pad = field.shape[1]
    xs_ref[...] = product(field, high_ref, low_ref, slice(0, 2 * pad)).reshape(cols, dips, 2 * pad)
    tail = lane_blocks(freqs)[-1][0]
    ys_ref[:, tail:pad] = jnp.zeros((sensors, pad - tail), F32)
    ys_ref[:, pad + tail :] = jnp.zeros((sensors, pad - tail), F32)
    height = min(32, sensors)
    for start, width in lane_blocks(freqs):
        for top in range(0, sensors, height):

            def column(c, acc):
                real, imag = acc
                for d in range(dips):
                    kr = k_ref[0, c, d, top : top + height, start : start + width]
                    ki = k_ref[1, c, d, top : top + height, start : start + width]
                    xr = xs_ref[c, d : d + 1, start : start + width]
                    xi = xs_ref[c, d : d + 1, pad + start : pad + start + width]
                    real = real + kr * xr - ki * xi
                    imag = imag + kr * xi + ki * xr
                return real, imag

            zero = jnp.zeros((height, width), F32)
            real, imag = lax.fori_loop(0, cols, column, (zero, zero))
            ys_ref[top : top + height, start : start + width] = real
            ys_ref[top : top + height, pad + start : pad + start + width] = imag
    series = to_series(ys_ref[:, :pad], ys_ref[:, pad:], high_ref, low_ref, steps)
    tiles = pad // LANES
    for o in range(sensors // ROWS):
        for t in range(tiles):
            out_ref[o * tiles + t] = series[o * ROWS : (o + 1) * ROWS, t * LANES : (t + 1) * LANES]


def first_kernel(steps, s_ref, k_ref, high_ref, low_ref, out_ref, xs_ref, ys_ref):
    forward_map(s_ref[...], k_ref, high_ref, low_ref, xs_ref, ys_ref, out_ref, steps)


def stepped(s_ref, g_ref, sums_ref):
    sums = jnp.sum(sums_ref[...], axis=0)
    image_sq = sums[:, :1]
    grad_sq = sums[:, LANES // 2 : LANES // 2 + 1]
    alpha = grad_sq / (image_sq + 8.0 * LAMBDA_REG * grad_sq + TINY_TERM)
    return jnp.maximum(s_ref[...] - alpha * g_ref[...], 0.0)


def step_kernel(steps, s_ref, g_ref, sums_ref, k_ref, high_ref, low_ref, out_ref, new_ref, xs_ref, ys_ref):
    new = stepped(s_ref, g_ref, sums_ref)
    new_ref[...] = new
    forward_map(new, k_ref, high_ref, low_ref, xs_ref, ys_ref, out_ref, steps)


def last_kernel(s_ref, g_ref, sums_ref, out_ref):
    new = stepped(s_ref, g_ref, sums_ref)
    cols, dips, steps = out_ref.shape
    for c in range(cols):
        out_ref[c] = new[c * dips : (c + 1) * dips, :steps]


def misfit_kernel(parts_ref, observed_ref, out_ref):
    misfit = jnp.sum(parts_ref[...], axis=0) - observed_ref[...]
    out_ref[...] = jnp.broadcast_to(misfit[None], out_ref.shape)


def adjoint_kernel(steps, r_ref, k_ref, high_ref, low_ref, out_ref, res_ref, ys_ref, xs_ref):
    _, cols, dips, sensors, freqs = k_ref.shape
    pad = xs_ref.shape[2] // 2
    tiles = pad // LANES
    for o in range(sensors // ROWS):
        for t in range(tiles):
            width = min(LANES, steps - t * LANES)
            res_ref[o * ROWS : (o + 1) * ROWS, t * LANES : t * LANES + width] = r_ref[o * tiles + t][:, :width]
    rows = [
        jnp.concatenate([r_ref[o * tiles + t] for t in range(tiles)], axis=1)
        for o in range(sensors // ROWS)
    ]
    misfit = jnp.concatenate(rows, axis=0)
    ys_ref[...] = product(misfit, high_ref, low_ref, slice(0, 2 * pad))
    tail = lane_blocks(freqs)[-1][0]
    xs_ref[:, :, tail:pad] = jnp.zeros((cols, dips, pad - tail), F32)
    xs_ref[:, :, pad + tail :] = jnp.zeros((cols, dips, pad - tail), F32)
    for start, width in lane_blocks(freqs):
        rr = [ys_ref[top : top + ROWS, start : start + width] for top in range(0, sensors, ROWS)]
        ri = [ys_ref[top : top + ROWS, pad + start : pad + start + width] for top in range(0, sensors, ROWS)]

        def column(c, carry):
            for d in range(dips):
                real = jnp.zeros((ROWS, width), F32)
                imag = jnp.zeros((ROWS, width), F32)
                for i in range(sensors // ROWS):
                    kr = k_ref[0, c, d, i * ROWS : (i + 1) * ROWS, start : start + width]
                    ki = k_ref[1, c, d, i * ROWS : (i + 1) * ROWS, start : start + width]
                    real = real + kr * rr[i] + ki * ri[i]
                    imag = imag + kr * ri[i] - ki * rr[i]
                xs_ref[c, d : d + 1, start : start + width] = jnp.sum(real, axis=0, keepdims=True)
                xs_ref[c, d : d + 1, pad + start : pad + start + width] = jnp.sum(imag, axis=0, keepdims=True)
            return carry

        lax.fori_loop(0, cols, column, 0)
    spectra = xs_ref[...].reshape(cols * dips, 2 * pad)
    series = to_series(spectra[:, :pad], spectra[:, pad:], high_ref, low_ref, steps)
    for i in range(out_ref.shape[0]):
        out_ref[i] = series


def gradient_kernel(
    steps, parts_ref, s_ref, below_ref, above_ref, k_ref, high_ref, low_ref, out_ref, g_ref, xs_ref, ys_ref
):
    cols, dips = k_ref.shape[1:3]
    field = s_ref[...]
    count = cols * dips
    earlier = jnp.concatenate([below_ref[...], field[: count - dips]], axis=0)
    later = jnp.concatenate([field[dips:], above_ref[...]], axis=0)
    dip = lax.broadcasted_iota(jnp.int32, field.shape, 0) % dips
    upper = jnp.where(dip == 0, 0.0, pltpu.roll(field, 1, 0))
    lower = jnp.where(dip == dips - 1, 0.0, pltpu.roll(field, count - 1, 0))
    smooth = 4.0 * field - (earlier + later) - lower - upper
    gradient = jnp.sum(parts_ref[...], axis=0) + LAMBDA_REG * smooth
    g_ref[...] = gradient
    forward_map(gradient, k_ref, high_ref, low_ref, xs_ref, ys_ref, out_ref, steps)


def squares_kernel(copies, parts_ref, g_ref, out_ref):
    image = jnp.sum(parts_ref[...], axis=0)
    gradient = g_ref[...]
    image_sq = jnp.sum(image * image, keepdims=True)
    grad_sq = jnp.sum(gradient * gradient, keepdims=True) * (1.0 / copies)
    lane = lax.broadcasted_iota(jnp.int32, (1, LANES), 1)
    both = jnp.where(lane < LANES // 2, image_sq, grad_sq)
    out_ref[...] = jnp.broadcast_to(both[None], out_ref.shape)


def shape(*dims):
    return jax.ShapeDtypeStruct(dims, F32)


def call(kernel, out_shape, scratch=()):
    return pl.pallas_call(
        kernel,
        out_shape=out_shape,
        scratch_shapes=[pltpu.VMEM(dims, F32) for dims in scratch],
        compiler_params=pltpu.CompilerParams(vmem_limit_bytes=VMEM_LIMIT),
    )


def body(kernel_spec, observed, initial):
    _, cols, dips, sensors, freqs = kernel_spec.shape
    steps = observed.shape[1]
    points = cols * dips
    pad = -(-freqs // LANES) * LANES
    tiles = pad // LANES
    params = lax.axis_size("param")
    groups = lax.axis_size("sensor")
    assert params == sensors // ROWS * tiles and dips == ROWS
    high, low = (jnp.asarray(part) for part in dft_table(steps, freqs, pad))
    me = lax.axis_index("param")
    own = lax.dynamic_slice(
        jnp.pad(observed, ((0, 0), (0, pad - steps))),
        (me // tiles * ROWS, me % tiles * LANES),
        (ROWS, LANES),
    )
    tiled = shape(params, ROWS, LANES)
    both = [(cols, dips, 2 * pad), (sensors, 2 * pad)]
    swap = functools.partial(lax.all_to_all, split_axis=0, concat_axis=0)
    up = [(i, i + 1) for i in range(params - 1)]
    down = [(i + 1, i) for i in range(params - 1)]

    sources = jnp.pad(initial.reshape(points, steps), ((0, 0), (0, pad - steps)))
    for iteration in range(ITERS):
        if iteration == 0:
            parts = call(functools.partial(first_kernel, steps), tiled, both)(sources, kernel_spec, high, low)
        else:
            parts, sources = call(
                functools.partial(step_kernel, steps), (tiled, shape(points, pad)), both
            )(sources, gradient, sums, kernel_spec, high, low)
        below = lax.ppermute(sources[points - dips :], "param", up)
        above = lax.ppermute(sources[:dips], "param", down)
        misfit = call(misfit_kernel, tiled)(swap(parts, "param"), own)
        partial, residual = call(
            functools.partial(adjoint_kernel, steps),
            (shape(groups, points, pad), shape(sensors, steps)),
            both[::-1],
        )(swap(misfit, "param"), kernel_spec, high, low)
        image, gradient = call(
            functools.partial(gradient_kernel, steps), (tiled, shape(points, pad)), both
        )(swap(partial, "sensor"), sources, below, above, kernel_spec, high, low)
        squares = call(functools.partial(squares_kernel, groups), shape(params * groups, 1, LANES))(
            swap(image, "param"), gradient
        )
        sums = swap(squares, ("param", "sensor"))
    sources = call(last_kernel, shape(cols, dips, steps))(sources, gradient, sums)
    return (sources, residual)


def solution(mesh):
    placed = (P(None, "param", None, "sensor", None), P("sensor", None), P("param", None, None))
    return jax.shard_map(
        body,
        mesh=mesh,
        in_specs=placed,
        out_specs=(P("param", None, None), P("sensor", None)),
        check_vma=False,
    )
```

```python
import functools
import math

import jax
import jax.numpy as jnp
import numpy as np
from jax import lax
from jax.experimental import pallas as pl
from jax.experimental.pallas import tpu as pltpu
from jax.sharding import PartitionSpec as P

ITERS = 2
LAMBDA_REG = 0.5
TINY_TERM = 1e-06
LANES = 128
ROWS = 8
F32 = jnp.float32
BF16 = jnp.bfloat16
VMEM_LIMIT = 20 * 1024 * 1024


def dft_table(steps, freqs, pad):
    index = np.arange(pad, dtype=np.int64)
    phase = (index[:, None] * index[None, :]) % (2 * steps)
    angle = phase * (math.pi / steps)
    inside = (index[:, None] < freqs) & (index[None, :] < freqs)
    whole = np.concatenate(
        [np.where(inside, np.cos(angle), 0.0), np.where(inside, -np.sin(angle), 0.0)], axis=1
    )
    high = whole.astype(np.float32).astype(BF16)
    low = (whole - high.astype(np.float64)).astype(np.float32).astype(BF16)
    return high, low


def product(x, high_ref, low_ref, columns):
    rows = x.shape[0]
    high = x.astype(BF16).astype(F32)
    terms = jnp.concatenate([high, x - high], axis=0).astype(BF16)
    dot = functools.partial(jnp.dot, preferred_element_type=F32)
    main = dot(terms, high_ref[:, columns])
    return main[:rows] + main[rows:] + dot(high.astype(BF16), low_ref[:, columns])


def to_series(real_part, imag_part, high_ref, low_ref, steps):
    pad = real_part.shape[1]
    column = lax.broadcasted_iota(jnp.int32, (1, pad), 1)
    weight = jnp.where((column == 0) | (column == steps), 1.0, 2.0) / (2.0 * steps)
    out = product(real_part * weight, high_ref, low_ref, slice(0, pad))
    out += product(imag_part * weight, high_ref, low_ref, slice(pad, 2 * pad))
    return jnp.where(column < steps, out, 0.0)


def lane_blocks(freqs):
    return [(start, min(LANES, freqs - start)) for start in range(0, freqs, LANES)]


def column_copy(c, k_any, k_ref, sems):
    return pltpu.make_async_copy(k_any.at[:, c], k_ref.at[:, c], sems.at[c])


def start_columns(k_any, k_ref, sems):
    for c in range(k_ref.shape[1] if sems is not None else 0):
        column_copy(c, k_any, k_ref, sems).start()


def forward_map(field, k_any, high_ref, low_ref, out_ref, xs_ref, ys_ref, k_ref, sems, steps):
    _, cols, dips, sensors, freqs = k_ref.shape
    pad = field.shape[1]
    xs_ref[...] = product(field, high_ref, low_ref, slice(0, 2 * pad)).reshape(cols, dips, 2 * pad)
    ys_ref[...] = jnp.zeros_like(ys_ref)
    height = min(32, sensors)

    def column(c, carry):
        if sems is not None:
            column_copy(c, k_any, k_ref, sems).wait()
        for start, width in lane_blocks(freqs):
            for top in range(0, sensors, height):
                rows = slice(top, top + height)
                rr = ys_ref[rows, start : start + width]
                ri = ys_ref[rows, pad + start : pad + start + width]
                ii = ir = jnp.zeros((height, width), F32)
                for d in range(dips):
                    kr = k_ref[0, c, d, rows, start : start + width]
                    ki = k_ref[1, c, d, rows, start : start + width]
                    xr = xs_ref[c, d : d + 1, start : start + width]
                    xi = xs_ref[c, d : d + 1, pad + start : pad + start + width]
                    rr = rr + kr * xr
                    ii = ii + ki * xi
                    ri = ri + kr * xi
                    ir = ir + ki * xr
                ys_ref[rows, start : start + width] = rr - ii
                ys_ref[rows, pad + start : pad + start + width] = ri + ir
        return carry

    lax.fori_loop(0, cols, column, 0)
    series = to_series(ys_ref[:, :pad], ys_ref[:, pad:], high_ref, low_ref, steps)
    tiles = pad // LANES
    for o in range(sensors // ROWS):
        for t in range(tiles):
            out_ref[o * tiles + t] = series[o * ROWS : (o + 1) * ROWS, t * LANES : (t + 1) * LANES]


def store_edges(field, dips, inner_ref, outer_ref):
    even = lax.axis_index("param") % 2 == 0
    first, last = field[:dips], field[field.shape[0] - dips :]
    inner_ref[...] = jnp.where(even, last, first)
    outer_ref[...] = jnp.where(even, first, last)


def first_kernel(
    steps,
    s_any,
    k_any,
    high_any,
    low_any,
    out_ref,
    padded_ref,
    inner_ref,
    outer_ref,
    xs_ref,
    ys_ref,
    k_ref,
    sems,
    high_ref,
    low_ref,
    s_ref,
    table_sems,
):
    tables = [
        pltpu.make_async_copy(high_any, high_ref, table_sems.at[0]),
        pltpu.make_async_copy(low_any, low_ref, table_sems.at[1]),
    ]
    initial = pltpu.make_async_copy(s_any, s_ref, table_sems.at[2])
    initial.start()
    for copy in tables:
        copy.start()
    start_columns(k_any, k_ref, sems)
    cols, dips, _ = s_ref.shape
    padded_ref[...] = jnp.zeros_like(padded_ref)
    initial.wait()
    for c in range(cols):
        padded_ref[c * dips : (c + 1) * dips, :steps] = s_ref[c]
    store_edges(padded_ref[...], dips, inner_ref, outer_ref)
    for copy in tables:
        copy.wait()
    forward_map(padded_ref[...], k_any, high_ref, low_ref, out_ref, xs_ref, ys_ref, k_ref, sems, steps)


def stepped(s_ref, g_ref, sums_ref):
    sums = jnp.sum(sums_ref[...], axis=0)
    image_sq = sums[:, :1]
    grad_sq = sums[:, LANES // 2 : LANES // 2 + 1]
    alpha = grad_sq / (image_sq + 8.0 * LAMBDA_REG * grad_sq + TINY_TERM)
    return jnp.maximum(s_ref[...] - alpha * g_ref[...], 0.0)


def step_kernel(s_ref, g_ref, sums_ref, new_ref, inner_ref, outer_ref):
    new = stepped(s_ref, g_ref, sums_ref)
    new_ref[...] = new
    store_edges(new, inner_ref.shape[0], inner_ref, outer_ref)


def map_kernel(steps, s_ref, k_ref, high_ref, low_ref, out_ref, xs_ref, ys_ref):
    forward_map(s_ref[...], None, high_ref, low_ref, out_ref, xs_ref, ys_ref, k_ref, None, steps)


def last_kernel(s_ref, g_ref, sums_ref, out_ref):
    new = stepped(s_ref, g_ref, sums_ref)
    cols, dips, steps = out_ref.shape
    for c in range(cols):
        out_ref[c] = new[c * dips : (c + 1) * dips, :steps]


def misfit_kernel(parts_ref, observed_ref, out_ref, padded_ref):
    steps = observed_ref.shape[1]
    tiles = padded_ref.shape[1] // LANES
    me = lax.axis_index("param")
    padded_ref[...] = jnp.zeros_like(padded_ref)
    padded_ref[:, :steps] = observed_ref[pl.ds(pl.multiple_of(me // tiles * ROWS, ROWS), ROWS), :]
    misfit = jnp.sum(parts_ref[...], axis=0)
    for t in range(tiles):
        misfit -= jnp.where(me % tiles == t, padded_ref[:, t * LANES : (t + 1) * LANES], 0.0)
    out_ref[...] = jnp.broadcast_to(misfit[None], out_ref.shape)


def packed(series, cols, steps):
    whole = steps // LANES
    width = steps - whole * LANES
    tiles = []
    tail = None
    for c in range(cols):
        rows = series[c * ROWS : (c + 1) * ROWS]
        tiles += [rows[:, t * LANES : (t + 1) * LANES] for t in range(whole)]
        end = rows[:, whole * LANES :]
        tail = end if tail is None else tail + pltpu.roll(end, c * width, 1)
    return tiles + [tail]


def unpacked(tiles, cols, steps):
    whole = steps // LANES
    width = steps - whole * LANES
    lane = lax.broadcasted_iota(jnp.int32, (ROWS, LANES), 1)
    tail = tiles[cols * whole]
    rows = []
    for c in range(cols):
        end = pltpu.roll(tail, LANES - c * width, 1) if c else tail
        parts = [tiles[c * whole + t] for t in range(whole)] + [jnp.where(lane < width, end, 0.0)]
        rows.append(jnp.concatenate(parts, axis=1))
    return jnp.concatenate(rows, axis=0)


def adjoint_kernel(steps, r_ref, k_ref, high_ref, low_ref, out_ref, res_ref, xs_ref, ys_ref):
    _, cols, dips, sensors, freqs = k_ref.shape
    pad = xs_ref.shape[2] // 2
    tiles = pad // LANES
    rows = [
        jnp.concatenate([r_ref[o * tiles + t] for t in range(tiles)], axis=1)
        for o in range(sensors // ROWS)
    ]
    misfit = jnp.concatenate(rows, axis=0)
    res_ref[...] = misfit[:, :steps]
    ys_ref[...] = product(misfit, high_ref, low_ref, slice(0, 2 * pad))
    xs_ref[...] = jnp.zeros_like(xs_ref)

    def column(c, carry):
        for start, width in lane_blocks(freqs):
            rr = [ys_ref[top : top + ROWS, start : start + width] for top in range(0, sensors, ROWS)]
            ri = [ys_ref[top : top + ROWS, pad + start : pad + start + width] for top in range(0, sensors, ROWS)]
            for d in range(dips):
                real = jnp.zeros((ROWS, width), F32)
                imag = jnp.zeros((ROWS, width), F32)
                for i in range(sensors // ROWS):
                    kr = k_ref[0, c, d, i * ROWS : (i + 1) * ROWS, start : start + width]
                    ki = k_ref[1, c, d, i * ROWS : (i + 1) * ROWS, start : start + width]
                    real = real + (kr * rr[i] + ki * ri[i])
                    imag = imag + (kr * ri[i] - ki * rr[i])
                xs_ref[c, d : d + 1, start : start + width] = jnp.sum(real, axis=0, keepdims=True)
                xs_ref[c, d : d + 1, pad + start : pad + start + width] = jnp.sum(imag, axis=0, keepdims=True)
        return carry

    lax.fori_loop(0, cols, column, 0)
    spectra = xs_ref[...].reshape(cols * dips, 2 * pad)
    series = to_series(spectra[:, :pad], spectra[:, pad:], high_ref, low_ref, steps)
    for j, tile in enumerate(packed(series, cols, steps)):
        for i in range(out_ref.shape[0]):
            out_ref[i, j] = tile


def gradient_kernel(
    steps, parts_ref, s_ref, inner_ref, outer_ref, k_ref, high_ref, low_ref, out_ref, g_ref, xs_ref, ys_ref
):
    cols, dips = k_ref.shape[1:3]
    field = s_ref[...]
    count = cols * dips
    even = lax.axis_index("param") % 2 == 0
    inner, outer = inner_ref[...], outer_ref[...]
    below, above = jnp.where(even, outer, inner), jnp.where(even, inner, outer)
    earlier = jnp.concatenate([below, field[: count - dips]], axis=0)
    later = jnp.concatenate([field[dips:], above], axis=0)
    dip = lax.broadcasted_iota(jnp.int32, field.shape, 0) % dips
    upper = jnp.where(dip == 0, 0.0, pltpu.roll(field, 1, 0))
    lower = jnp.where(dip == dips - 1, 0.0, pltpu.roll(field, count - 1, 0))
    smooth = 4.0 * field - (earlier + later) - lower - upper
    summed = jnp.sum(parts_ref[...], axis=0)
    back = unpacked([summed[j] for j in range(summed.shape[0])], cols, steps)
    gradient = back + LAMBDA_REG * smooth
    g_ref[...] = gradient
    forward_map(gradient, None, high_ref, low_ref, out_ref, xs_ref, ys_ref, k_ref, None, steps)


def squares_kernel(copies, parts_ref, g_ref, out_ref):
    image = jnp.sum(parts_ref[...], axis=0)
    gradient = g_ref[...]
    image_sq = jnp.sum(image * image, keepdims=True)
    grad_sq = jnp.sum(gradient * gradient, keepdims=True) * (1.0 / copies)
    lane = lax.broadcasted_iota(jnp.int32, (1, LANES), 1)
    both = jnp.where(lane < LANES // 2, image_sq, grad_sq)
    out_ref[...] = jnp.broadcast_to(both[None], out_ref.shape)


def shape(*dims):
    return jax.ShapeDtypeStruct(dims, F32)


def call(kernel, out_shape, scratch=(), outside=(), inputs=0):
    specs = [pl.BlockSpec(memory_space=pltpu.HBM if i in outside else pltpu.VMEM) for i in range(inputs)]
    return pl.pallas_call(
        kernel,
        out_shape=out_shape,
        scratch_shapes=[pltpu.VMEM(dims, F32) if isinstance(dims, tuple) else dims for dims in scratch],
        compiler_params=pltpu.CompilerParams(vmem_limit_bytes=VMEM_LIMIT),
        **({"in_specs": specs} if inputs else {}),
    )


def body(kernel_spec, observed, initial):
    _, cols, dips, sensors, freqs = kernel_spec.shape
    steps = observed.shape[1]
    points = cols * dips
    pad = -(-freqs // LANES) * LANES
    tiles = pad // LANES
    params = lax.axis_size("param")
    groups = lax.axis_size("sensor")
    assert params == sensors // ROWS * tiles and dips == ROWS
    assert cols * (steps % LANES) <= LANES
    high, low = (jnp.asarray(part) for part in dft_table(steps, freqs, pad))
    tiled = shape(params, ROWS, LANES)
    field = shape(points, pad)
    work = [(cols, dips, 2 * pad), (sensors, 2 * pad), kernel_spec.shape, pltpu.SemaphoreType.DMA((cols,))]
    table = pltpu.VMEM(high.shape, BF16)
    swap = functools.partial(lax.all_to_all, split_axis=0, concat_axis=0)
    stay = functools.partial(pltpu.with_memory_space_constraint, memory_space=pltpu.HBM)
    spec = stay(kernel_spec)
    pairs = [(i, i ^ 1) for i in range(params)]
    others = [(i, i + 1 if i % 2 else i - 1) for i in range(1, params - 1)]
    edge = shape(dips, pad)
    map_work = work[:2]

    for iteration in range(ITERS):
        if iteration == 0:
            parts, sources, inner, outer = call(
                functools.partial(first_kernel, steps),
                (tiled, field, edge, edge),
                work + [table, table, pltpu.VMEM(initial.shape, F32), pltpu.SemaphoreType.DMA((3,))],
                outside=(0, 1, 2, 3),
                inputs=4,
            )(stay(initial), spec, stay(high), stay(low))
        else:
            sources, inner, outer = call(step_kernel, (field, edge, edge))(sources, gradient, sums)
            parts = call(functools.partial(map_kernel, steps), tiled, map_work)(
                sources, kernel_spec, high, low
            )
        inner, outer = lax.ppermute(inner, "param", pairs), lax.ppermute(outer, "param", others)
        if iteration == 0:
            parts, inner, outer = lax.optimization_barrier((swap(parts, "param"), inner, outer))
        else:
            parts, inner, outer = lax.optimization_barrier((parts, inner, outer))
            parts = swap(parts, "param")
        misfit = call(misfit_kernel, tiled, [(ROWS, pad)])(parts, observed)
        count = cols * (steps // LANES) + 1
        partial, residual = call(
            functools.partial(adjoint_kernel, steps),
            (shape(groups, count, ROWS, LANES), shape(sensors, steps)),
            map_work,
        )(swap(misfit, "param"), kernel_spec, high, low)
        image, gradient = call(functools.partial(gradient_kernel, steps), (tiled, field), map_work)(
            swap(partial, "sensor"), sources, inner, outer, kernel_spec, high, low
        )
        squares = call(functools.partial(squares_kernel, groups), shape(params * groups, 1, LANES))(
            swap(image, "param"), gradient
        )
        sums = swap(squares, ("param", "sensor"))
    sources = call(last_kernel, shape(cols, dips, steps))(sources, gradient, sums)
    return (sources, residual)


def solution(mesh):
    placed = (P(None, "param", None, "sensor", None), P("sensor", None), P("param", None, None))
    return jax.shard_map(
        body,
        mesh=mesh,
        in_specs=placed,
        out_specs=(P("param", None, None), P("sensor", None)),
        check_vma=False,
    )
```

```python
import functools
import math

import jax
import jax.numpy as jnp
import numpy as np
from jax import lax
from jax.experimental import pallas as pl
from jax.experimental.pallas import tpu as pltpu
from jax.sharding import PartitionSpec as P

ITERS = 2
LAMBDA_REG = 0.5
TINY_TERM = 1e-06
LANES = 128
ROWS = 8
F32 = jnp.float32
BF16 = jnp.bfloat16
VMEM_LIMIT = 20 * 1024 * 1024


def dft_table(steps, freqs, pad):
    index = np.arange(pad, dtype=np.int64)
    phase = (index[:, None] * index[None, :]) % (2 * steps)
    angle = phase * (math.pi / steps)
    inside = (index[:, None] < freqs) & (index[None, :] < freqs)
    whole = np.concatenate(
        [np.where(inside, np.cos(angle), 0.0), np.where(inside, -np.sin(angle), 0.0)], axis=1
    )
    high = whole.astype(np.float32).astype(BF16)
    low = (whole - high.astype(np.float64)).astype(np.float32).astype(BF16)
    return high, low


def product(x, high_ref, low_ref, columns):
    rows = x.shape[0]
    high = x.astype(BF16).astype(F32)
    terms = jnp.concatenate([high, x - high], axis=0).astype(BF16)
    dot = functools.partial(jnp.dot, preferred_element_type=F32)
    main = dot(terms, high_ref[:, columns])
    return main[:rows] + main[rows:] + dot(high.astype(BF16), low_ref[:, columns])


def to_series(real_part, imag_part, high_ref, low_ref, steps):
    pad = real_part.shape[1]
    column = lax.broadcasted_iota(jnp.int32, (1, pad), 1)
    weight = jnp.where((column == 0) | (column == steps), 1.0, 2.0) / (2.0 * steps)
    out = product(real_part * weight, high_ref, low_ref, slice(0, pad))
    out += product(imag_part * weight, high_ref, low_ref, slice(pad, 2 * pad))
    return jnp.where(column < steps, out, 0.0)


def lane_blocks(freqs):
    return [(start, min(LANES, freqs - start)) for start in range(0, freqs, LANES)]


def column_copy(c, k_any, k_ref, sems):
    return pltpu.make_async_copy(k_any.at[:, c], k_ref.at[:, c], sems.at[c])


def start_columns(k_any, k_ref, sems):
    for c in range(k_ref.shape[1] if sems is not None else 0):
        column_copy(c, k_any, k_ref, sems).start()


def forward_map(field, k_any, high_ref, low_ref, out_ref, xs_ref, ys_ref, k_ref, sems, steps):
    _, cols, dips, sensors, freqs = k_ref.shape
    pad = field.shape[1]
    xs_ref[...] = product(field, high_ref, low_ref, slice(0, 2 * pad)).reshape(cols, dips, 2 * pad)
    ys_ref[...] = jnp.zeros_like(ys_ref)
    height = min(32, sensors)

    def column(c, carry):
        if sems is not None:
            column_copy(c, k_any, k_ref, sems).wait()
        for start, width in lane_blocks(freqs):
            for top in range(0, sensors, height):
                rows = slice(top, top + height)
                rr = ys_ref[rows, start : start + width]
                ri = ys_ref[rows, pad + start : pad + start + width]
                ii = ir = jnp.zeros((height, width), F32)
                for d in range(dips):
                    kr = k_ref[0, c, d, rows, start : start + width]
                    ki = k_ref[1, c, d, rows, start : start + width]
                    xr = xs_ref[c, d : d + 1, start : start + width]
                    xi = xs_ref[c, d : d + 1, pad + start : pad + start + width]
                    rr = rr + kr * xr
                    ii = ii + ki * xi
                    ri = ri + kr * xi
                    ir = ir + ki * xr
                ys_ref[rows, start : start + width] = rr - ii
                ys_ref[rows, pad + start : pad + start + width] = ri + ir
        return carry

    lax.fori_loop(0, cols, column, 0)
    series = to_series(ys_ref[:, :pad], ys_ref[:, pad:], high_ref, low_ref, steps)
    tiles = pad // LANES
    for o in range(sensors // ROWS):
        for t in range(tiles):
            out_ref[o * tiles + t] = series[o * ROWS : (o + 1) * ROWS, t * LANES : (t + 1) * LANES]


def store_edges(field, dips, inner_ref, outer_ref):
    even = lax.axis_index("param") % 2 == 0
    first, last = field[:dips], field[field.shape[0] - dips :]
    inner_ref[...] = jnp.where(even, last, first)
    outer_ref[...] = jnp.where(even, first, last)


def first_kernel(
    steps,
    s_any,
    k_any,
    high_any,
    low_any,
    out_ref,
    padded_ref,
    inner_ref,
    outer_ref,
    high_ref,
    low_ref,
    xs_ref,
    ys_ref,
    k_ref,
    sems,
    s_ref,
    table_sems,
):
    tables = [
        pltpu.make_async_copy(high_any, high_ref, table_sems.at[0]),
        pltpu.make_async_copy(low_any, low_ref, table_sems.at[1]),
    ]
    initial = pltpu.make_async_copy(s_any, s_ref, table_sems.at[2])
    initial.start()
    for copy in tables:
        copy.start()
    start_columns(k_any, k_ref, sems)
    cols, dips, _ = s_ref.shape
    padded_ref[...] = jnp.zeros_like(padded_ref)
    initial.wait()
    for c in range(cols):
        padded_ref[c * dips : (c + 1) * dips, :steps] = s_ref[c]
    store_edges(padded_ref[...], dips, inner_ref, outer_ref)
    for copy in tables:
        copy.wait()
    forward_map(padded_ref[...], k_any, high_ref, low_ref, out_ref, xs_ref, ys_ref, k_ref, sems, steps)


def step_size(sums_ref):
    sums = jnp.sum(sums_ref[...], axis=0)
    image_sq = sums[:, :1]
    grad_sq = sums[:, LANES // 4 : LANES // 4 + 1]
    return grad_sq / (image_sq + 8.0 * LAMBDA_REG * grad_sq + TINY_TERM)


def stepped(field, gradient, alpha):
    return jnp.maximum(field - alpha * gradient, 0.0)


def gathered_row(sums_ref, neighbour, exists, groups):
    lane = lax.broadcasted_iota(jnp.int32, (1, LANES), 1)
    start = jnp.where(exists, neighbour, 0) * groups
    tiles = []
    for i in range(0, groups, 2):
        low, high = sums_ref[start + i], sums_ref[start + i + 1]
        tiles.append(jnp.where(lane < LANES // 2, pltpu.roll(low, LANES // 2, 1), high))
    return jnp.where(exists, jnp.concatenate(tiles, axis=1), 0.0)


def step_kernel(
    steps,
    params,
    groups,
    s_ref,
    g_ref,
    sums_ref,
    inner_ref,
    outer_ref,
    k_ref,
    high_ref,
    low_ref,
    out_ref,
    new_ref,
    new_inner_ref,
    new_outer_ref,
    xs_ref,
    ys_ref,
):
    me = lax.axis_index("param")
    even = me % 2 == 0
    alpha = step_size(sums_ref)
    new = stepped(s_ref[...], g_ref[...], alpha)
    new_ref[...] = new
    below = gathered_row(sums_ref, me - 1, me > 0, groups)
    above = gathered_row(sums_ref, me + 1, me < params - 1, groups)
    new_inner_ref[...] = stepped(inner_ref[...], jnp.where(even, above, below), alpha)
    new_outer_ref[...] = stepped(outer_ref[...], jnp.where(even, below, above), alpha)
    forward_map(new, None, high_ref, low_ref, out_ref, xs_ref, ys_ref, k_ref, None, steps)


def last_kernel(s_ref, g_ref, sums_ref, out_ref):
    new = stepped(s_ref[...], g_ref[...], step_size(sums_ref))
    cols, dips, steps = out_ref.shape
    for c in range(cols):
        out_ref[c] = new[c * dips : (c + 1) * dips, :steps]


def misfit_kernel(parts_ref, observed_ref, out_ref, padded_ref):
    steps = observed_ref.shape[1]
    tiles = padded_ref.shape[1] // LANES
    me = lax.axis_index("param")
    padded_ref[...] = jnp.zeros_like(padded_ref)
    padded_ref[:, :steps] = observed_ref[pl.ds(pl.multiple_of(me // tiles * ROWS, ROWS), ROWS), :]
    misfit = jnp.sum(parts_ref[...], axis=0)
    for t in range(tiles):
        misfit -= jnp.where(me % tiles == t, padded_ref[:, t * LANES : (t + 1) * LANES], 0.0)
    out_ref[...] = jnp.broadcast_to(misfit[None], out_ref.shape)


def packed(series, cols, steps):
    whole = steps // LANES
    width = steps - whole * LANES
    tiles = []
    tail = None
    for c in range(cols):
        rows = series[c * ROWS : (c + 1) * ROWS]
        tiles += [rows[:, t * LANES : (t + 1) * LANES] for t in range(whole)]
        end = rows[:, whole * LANES :]
        tail = end if tail is None else tail + pltpu.roll(end, c * width, 1)
    return tiles + [tail]


def unpacked(tiles, cols, steps):
    whole = steps // LANES
    width = steps - whole * LANES
    lane = lax.broadcasted_iota(jnp.int32, (ROWS, LANES), 1)
    tail = tiles[cols * whole]
    rows = []
    for c in range(cols):
        end = pltpu.roll(tail, LANES - c * width, 1) if c else tail
        parts = [tiles[c * whole + t] for t in range(whole)] + [jnp.where(lane < width, end, 0.0)]
        rows.append(jnp.concatenate(parts, axis=1))
    return jnp.concatenate(rows, axis=0)


def adjoint_kernel(
    steps, r_ref, inner_ref, outer_ref, k_ref, high_ref, low_ref, out_ref, res_ref, xs_ref, ys_ref, k_any=None, sems=None
):
    start_columns(k_any, k_ref, sems)
    _, cols, dips, sensors, freqs = k_ref.shape
    pad = xs_ref.shape[2] // 2
    tiles = pad // LANES
    rows = [
        jnp.concatenate([r_ref[o * tiles + t] for t in range(tiles)], axis=1)
        for o in range(sensors // ROWS)
    ]
    misfit = jnp.concatenate(rows, axis=0)
    res_ref[...] = misfit[:, :steps]
    ys_ref[...] = product(misfit, high_ref, low_ref, slice(0, 2 * pad))
    xs_ref[...] = jnp.zeros_like(xs_ref)

    def column(c, carry):
        if sems is not None:
            column_copy(c, k_any, k_ref, sems).wait()
        for start, width in lane_blocks(freqs):
            rr = [ys_ref[top : top + ROWS, start : start + width] for top in range(0, sensors, ROWS)]
            ri = [ys_ref[top : top + ROWS, pad + start : pad + start + width] for top in range(0, sensors, ROWS)]
            for d in range(dips):
                real = jnp.zeros((ROWS, width), F32)
                imag = jnp.zeros((ROWS, width), F32)
                for i in range(sensors // ROWS):
                    kr = k_ref[0, c, d, i * ROWS : (i + 1) * ROWS, start : start + width]
                    ki = k_ref[1, c, d, i * ROWS : (i + 1) * ROWS, start : start + width]
                    real = real + (kr * rr[i] + ki * ri[i])
                    imag = imag + (kr * ri[i] - ki * rr[i])
                xs_ref[c, d : d + 1, start : start + width] = jnp.sum(real, axis=0, keepdims=True)
                xs_ref[c, d : d + 1, pad + start : pad + start + width] = jnp.sum(imag, axis=0, keepdims=True)
        return carry

    lax.fori_loop(0, cols, column, 0)
    spectra = xs_ref[...].reshape(cols * dips, 2 * pad)
    series = to_series(spectra[:, :pad], spectra[:, pad:], high_ref, low_ref, steps)
    even = lax.axis_index("param") % 2 == 0
    inner, outer = inner_ref[...], outer_ref[...]
    mine = lax.broadcasted_iota(jnp.int32, inner.shape, 0) == lax.axis_index("sensor")
    below = jnp.where(mine, jnp.where(even, outer, inner), 0.0)
    above = jnp.where(mine, jnp.where(even, inner, outer), 0.0)
    inside = jnp.zeros(((cols - 2) * dips, pad), F32)
    series -= LAMBDA_REG * jnp.concatenate([below, inside, above], axis=0)
    for j, tile in enumerate(packed(series, cols, steps)):
        for i in range(out_ref.shape[0]):
            out_ref[i, j] = tile


def first_adjoint_kernel(
    steps, r_ref, inner_ref, outer_ref, k_any, high_ref, low_ref, out_ref, res_ref, k_ref, xs_ref, ys_ref, sems
):
    adjoint_kernel(
        steps, r_ref, inner_ref, outer_ref, k_ref, high_ref, low_ref, out_ref, res_ref, xs_ref, ys_ref, k_any, sems
    )


def gradient_kernel(
    steps, parts_ref, s_ref, k_ref, high_ref, low_ref, out_ref, g_ref, xs_ref, ys_ref
):
    cols, dips = k_ref.shape[1:3]
    field = s_ref[...]
    count = cols * dips
    edge = jnp.zeros((dips, field.shape[1]), F32)
    earlier = jnp.concatenate([edge, field[: count - dips]], axis=0)
    later = jnp.concatenate([field[dips:], edge], axis=0)
    dip = lax.broadcasted_iota(jnp.int32, field.shape, 0) % dips
    upper = jnp.where(dip == 0, 0.0, pltpu.roll(field, 1, 0))
    lower = jnp.where(dip == dips - 1, 0.0, pltpu.roll(field, count - 1, 0))
    smooth = 4.0 * field - (earlier + later) - lower - upper
    summed = jnp.sum(parts_ref[...], axis=0)
    back = unpacked([summed[j] for j in range(summed.shape[0])], cols, steps)
    gradient = back + LAMBDA_REG * smooth
    g_ref[...] = gradient
    forward_map(gradient, None, high_ref, low_ref, out_ref, xs_ref, ys_ref, k_ref, None, steps)


def squares_kernel(params, groups, parts_ref, g_ref, out_ref):
    image = jnp.sum(parts_ref[...], axis=0)
    gradient = g_ref[...]
    image_sq = jnp.sum(image * image, keepdims=True)
    grad_sq = jnp.sum(gradient * gradient, keepdims=True) * (1.0 / groups)
    lane = lax.broadcasted_iota(jnp.int32, (1, LANES), 1)
    both = jnp.where(lane < LANES // 4, image_sq, grad_sq)
    out_ref[...] = jnp.broadcast_to(both[None], out_ref.shape)
    me, group = lax.axis_index("param"), lax.axis_index("sensor")
    points, pad = gradient.shape
    part = pad // groups

    def send(target, edge):
        tile = jnp.zeros((ROWS, LANES), F32)
        for t in range(pad // LANES):
            tile += jnp.where(group // 2 == t, edge[:, t * LANES : (t + 1) * LANES], 0.0)
        tile = jnp.where(group % 2 == 1, tile, pltpu.roll(tile, part, 1))
        rows = jnp.where(lane < part, both, tile)
        for i in range(groups):
            out_ref[target * groups + i] = rows[i : i + 1]

    @pl.when(me > 0)
    def _():
        send(me - 1, gradient[:ROWS])

    @pl.when(me < params - 1)
    def _():
        send(me + 1, gradient[points - ROWS :])


def shape(*dims):
    return jax.ShapeDtypeStruct(dims, F32)


def call(kernel, out_shape, scratch=(), outside=(), inputs=0):
    specs = [pl.BlockSpec(memory_space=pltpu.HBM if i in outside else pltpu.VMEM) for i in range(inputs)]
    return pl.pallas_call(
        kernel,
        out_shape=out_shape,
        scratch_shapes=[pltpu.VMEM(dims, F32) if isinstance(dims, tuple) else dims for dims in scratch],
        compiler_params=pltpu.CompilerParams(vmem_limit_bytes=VMEM_LIMIT),
        **({"in_specs": specs} if inputs else {}),
    )


def body(kernel_spec, observed, initial):
    _, cols, dips, sensors, freqs = kernel_spec.shape
    steps = observed.shape[1]
    points = cols * dips
    pad = -(-freqs // LANES) * LANES
    tiles = pad // LANES
    params = lax.axis_size("param")
    groups = lax.axis_size("sensor")
    assert params == sensors // ROWS * tiles and dips == ROWS
    assert cols * (steps % LANES) <= LANES and groups == dips and groups * LANES == 2 * pad
    high, low = (jnp.asarray(part) for part in dft_table(steps, freqs, pad))
    tiled = shape(params, ROWS, LANES)
    field = shape(points, pad)
    work = [(cols, dips, 2 * pad), (sensors, 2 * pad), kernel_spec.shape, pltpu.SemaphoreType.DMA((cols,))]
    swap = functools.partial(lax.all_to_all, split_axis=0, concat_axis=0)
    stay = functools.partial(pltpu.with_memory_space_constraint, memory_space=pltpu.HBM)
    spec = stay(kernel_spec)
    pairs = [(i, i ^ 1) for i in range(params)]
    others = [(i, i + 1 if i % 2 else i - 1) for i in range(1, params - 1)]
    edge = shape(dips, pad)
    map_work = work[:2]

    count = cols * (steps // LANES) + 1
    back = (shape(groups, count, ROWS, LANES), shape(sensors, steps))
    table = jax.ShapeDtypeStruct(high.shape, BF16)
    for iteration in range(ITERS):
        if iteration == 0:
            parts, sources, inner, outer, high, low = call(
                functools.partial(first_kernel, steps),
                (tiled, field, edge, edge, table, table),
                work + [pltpu.VMEM(initial.shape, F32), pltpu.SemaphoreType.DMA((3,))],
                outside=(0, 1, 2, 3),
                inputs=4,
            )(stay(initial), spec, stay(high), stay(low))
            inner, outer = lax.ppermute(inner, "param", pairs), lax.ppermute(outer, "param", others)
            parts, inner, outer = lax.optimization_barrier((swap(parts, "param"), inner, outer))
        else:
            parts, sources, inner, outer = call(
                functools.partial(step_kernel, steps, params, groups), (tiled, field, edge, edge), map_work
            )(sources, gradient, sums, inner, outer, held, high, low)
            parts = swap(parts, "param")
        misfit = swap(call(misfit_kernel, tiled, [(ROWS, pad)])(parts, observed), "param")
        if iteration == 0:
            partial, residual, held = call(
                functools.partial(first_adjoint_kernel, steps),
                back + (shape(*kernel_spec.shape),),
                map_work + work[3:],
                outside=(3,),
                inputs=6,
            )(misfit, inner, outer, spec, high, low)
        else:
            partial, residual = call(functools.partial(adjoint_kernel, steps), back, map_work)(
                misfit, inner, outer, held, high, low
            )
        image, gradient = call(functools.partial(gradient_kernel, steps), (tiled, field), map_work)(
            swap(partial, "sensor"), sources, held, high, low
        )
        squares = call(
            functools.partial(squares_kernel, params, groups), shape(params * groups, 1, LANES)
        )(swap(image, "param"), gradient)
        sums = swap(squares, ("param", "sensor"))
    sources = call(last_kernel, shape(cols, dips, steps))(sources, gradient, sums)
    return (sources, residual)


def solution(mesh):
    placed = (P(None, "param", None, "sensor", None), P("sensor", None), P("param", None, None))
    return jax.shard_map(
        body,
        mesh=mesh,
        in_specs=placed,
        out_specs=(P("param", None, None), P("sensor", None)),
        check_vma=False,
    )
```

```python
import functools
import math

import jax
import jax.numpy as jnp
import numpy as np
from jax import lax
from jax.experimental import pallas as pl
from jax.experimental.pallas import tpu as pltpu
from jax.sharding import PartitionSpec as P

ITERS = 2
LAMBDA_REG = 0.5
TINY_TERM = 1e-06
LANES = 128
ROWS = 8
F32 = jnp.float32
BF16 = jnp.bfloat16
VMEM_LIMIT = 20 * 1024 * 1024


def dft_table(steps, freqs, pad):
    index = np.arange(pad, dtype=np.int64)
    phase = (index[:, None] * index[None, :]) % (2 * steps)
    angle = phase * (math.pi / steps)
    inside = (index[:, None] < freqs) & (index[None, :] < freqs)
    whole = np.concatenate(
        [np.where(inside, np.cos(angle), 0.0), np.where(inside, -np.sin(angle), 0.0)], axis=1
    )
    high = whole.astype(np.float32).astype(BF16)
    low = (whole - high.astype(np.float64)).astype(np.float32).astype(BF16)
    return high, low


def product(x, high_ref, low_ref, columns):
    rows = x.shape[0]
    high = x.astype(BF16).astype(F32)
    terms = jnp.concatenate([high, x - high], axis=0).astype(BF16)
    dot = functools.partial(jnp.dot, preferred_element_type=F32)
    main = dot(terms, high_ref[:, columns])
    return main[:rows] + main[rows:] + dot(high.astype(BF16), low_ref[:, columns])


def to_series(real_part, imag_part, high_ref, low_ref, steps):
    pad = real_part.shape[1]
    column = lax.broadcasted_iota(jnp.int32, (1, pad), 1)
    weight = jnp.where((column == 0) | (column == steps), 1.0, 2.0) / (2.0 * steps)
    out = product(real_part * weight, high_ref, low_ref, slice(0, pad))
    out += product(imag_part * weight, high_ref, low_ref, slice(pad, 2 * pad))
    return jnp.where(column < steps, out, 0.0)


def lane_blocks(freqs):
    return [(start, min(LANES, freqs - start)) for start in range(0, freqs, LANES)]


def column_copy(c, k_any, k_ref, sems):
    return pltpu.make_async_copy(k_any.at[:, c], k_ref.at[:, c], sems.at[c])


def start_columns(k_any, k_ref, sems):
    for c in range(k_ref.shape[1] if sems is not None else 0):
        column_copy(c, k_any, k_ref, sems).start()


def forward_map(field, k_any, high_ref, low_ref, out_ref, xs_ref, ys_ref, k_ref, sems, steps):
    _, cols, dips, sensors, freqs = k_ref.shape
    pad = field.shape[1]
    xs_ref[...] = product(field, high_ref, low_ref, slice(0, 2 * pad)).reshape(cols, dips, 2 * pad)
    ys_ref[...] = jnp.zeros_like(ys_ref)
    height = min(8, sensors)

    def column(c, carry):
        if sems is not None:
            column_copy(c, k_any, k_ref, sems).wait()
        for start, width in lane_blocks(freqs):
            for top in range(0, sensors, height):
                rows = slice(top, top + height)
                real = ys_ref[rows, start : start + width]
                imag = ys_ref[rows, pad + start : pad + start + width]
                for d in range(dips):
                    kr = k_ref[0, c, d, rows, start : start + width]
                    ki = k_ref[1, c, d, rows, start : start + width]
                    xr = xs_ref[c, d : d + 1, start : start + width]
                    xi = xs_ref[c, d : d + 1, pad + start : pad + start + width]
                    real = real + (kr * xr - ki * xi)
                    imag = imag + (kr * xi + ki * xr)
                ys_ref[rows, start : start + width] = real
                ys_ref[rows, pad + start : pad + start + width] = imag
        return carry

    lax.fori_loop(0, cols, column, 0)
    series = to_series(ys_ref[:, :pad], ys_ref[:, pad:], high_ref, low_ref, steps)
    tiles = pad // LANES
    for o in range(sensors // ROWS):
        for t in range(tiles):
            out_ref[o * tiles + t] = series[o * ROWS : (o + 1) * ROWS, t * LANES : (t + 1) * LANES]


def store_edges(field, dips, inner_ref, outer_ref):
    even = lax.axis_index("param") % 2 == 0
    first, last = field[:dips], field[field.shape[0] - dips :]
    inner_ref[...] = jnp.where(even, last, first)
    outer_ref[...] = jnp.where(even, first, last)


def first_kernel(
    steps,
    s_any,
    k_any,
    high_any,
    low_any,
    out_ref,
    padded_ref,
    inner_ref,
    outer_ref,
    high_ref,
    low_ref,
    xs_ref,
    ys_ref,
    k_ref,
    sems,
    s_ref,
    table_sems,
):
    tables = [
        pltpu.make_async_copy(high_any, high_ref, table_sems.at[0]),
        pltpu.make_async_copy(low_any, low_ref, table_sems.at[1]),
    ]
    initial = pltpu.make_async_copy(s_any, s_ref, table_sems.at[2])
    initial.start()
    for copy in tables:
        copy.start()
    start_columns(k_any, k_ref, sems)
    cols, dips, _ = s_ref.shape
    padded_ref[...] = jnp.zeros_like(padded_ref)
    initial.wait()
    for c in range(cols):
        padded_ref[c * dips : (c + 1) * dips, :steps] = s_ref[c]
    store_edges(padded_ref[...], dips, inner_ref, outer_ref)
    for copy in tables:
        copy.wait()
    forward_map(padded_ref[...], k_any, high_ref, low_ref, out_ref, xs_ref, ys_ref, k_ref, sems, steps)


def step_size(sums_ref):
    sums = jnp.sum(jnp.sum(sums_ref[...], axis=0), axis=0, keepdims=True)
    image_sq = sums[:, :1]
    grad_sq = sums[:, LANES // 4 : LANES // 4 + 1]
    return grad_sq / (image_sq + 8.0 * LAMBDA_REG * grad_sq + TINY_TERM)


def stepped(field, gradient, alpha):
    return jnp.maximum(field - alpha * gradient, 0.0)


def gathered_row(sums_ref, neighbour, exists):
    lane = lax.broadcasted_iota(jnp.int32, (1, LANES), 1)
    came = sums_ref[jnp.where(exists, neighbour, 0)]
    turned = pltpu.roll(came, LANES // 2, 1)
    tiles = [
        jnp.where(lane < LANES // 2, turned[i : i + 1], came[i + 1 : i + 2]) for i in range(0, came.shape[0], 2)
    ]
    return jnp.where(exists, jnp.concatenate(tiles, axis=1), 0.0)


def step_kernel(
    steps,
    params,
    s_ref,
    g_ref,
    sums_ref,
    inner_ref,
    outer_ref,
    k_ref,
    high_ref,
    low_ref,
    out_ref,
    new_ref,
    new_inner_ref,
    new_outer_ref,
    xs_ref,
    ys_ref,
):
    me = lax.axis_index("param")
    even = me % 2 == 0
    alpha = step_size(sums_ref)
    new = stepped(s_ref[...], g_ref[...], alpha)
    new_ref[...] = new
    below = gathered_row(sums_ref, me - 1, me > 0)
    above = gathered_row(sums_ref, me + 1, me < params - 1)
    new_inner_ref[...] = stepped(inner_ref[...], jnp.where(even, above, below), alpha)
    new_outer_ref[...] = stepped(outer_ref[...], jnp.where(even, below, above), alpha)
    forward_map(new, None, high_ref, low_ref, out_ref, xs_ref, ys_ref, k_ref, None, steps)


def last_kernel(s_ref, g_ref, sums_ref, out_ref):
    new = stepped(s_ref[...], g_ref[...], step_size(sums_ref))
    cols, dips, steps = out_ref.shape
    for c in range(cols):
        out_ref[c] = new[c * dips : (c + 1) * dips, :steps]


def misfit_kernel(parts_ref, observed_ref, out_ref, padded_ref):
    steps = observed_ref.shape[1]
    tiles = padded_ref.shape[1] // LANES
    me = lax.axis_index("param")
    padded_ref[...] = jnp.zeros_like(padded_ref)
    padded_ref[:, :steps] = observed_ref[pl.ds(pl.multiple_of(me // tiles * ROWS, ROWS), ROWS), :]
    misfit = jnp.sum(parts_ref[...], axis=0)
    for t in range(tiles):
        misfit -= jnp.where(me % tiles == t, padded_ref[:, t * LANES : (t + 1) * LANES], 0.0)
    out_ref[...] = jnp.broadcast_to(misfit[None], out_ref.shape)


def packed(series, cols, steps):
    whole = steps // LANES
    width = steps - whole * LANES
    tiles = []
    tail = None
    for c in range(cols):
        rows = series[c * ROWS : (c + 1) * ROWS]
        tiles += [rows[:, t * LANES : (t + 1) * LANES] for t in range(whole)]
        end = rows[:, whole * LANES :]
        tail = end if tail is None else tail + pltpu.roll(end, c * width, 1)
    return tiles + [tail]


def unpacked(tiles, cols, steps):
    whole = steps // LANES
    width = steps - whole * LANES
    lane = lax.broadcasted_iota(jnp.int32, (ROWS, LANES), 1)
    tail = tiles[cols * whole]
    rows = []
    for c in range(cols):
        end = pltpu.roll(tail, LANES - c * width, 1) if c else tail
        parts = [tiles[c * whole + t] for t in range(whole)] + [jnp.where(lane < width, end, 0.0)]
        rows.append(jnp.concatenate(parts, axis=1))
    return jnp.concatenate(rows, axis=0)


def adjoint_kernel(
    steps, r_ref, inner_ref, outer_ref, k_ref, high_ref, low_ref, out_ref, res_ref, xs_ref, ys_ref, k_any=None, sems=None
):
    start_columns(k_any, k_ref, sems)
    _, cols, dips, sensors, freqs = k_ref.shape
    pad = xs_ref.shape[2] // 2
    tiles = pad // LANES
    rows = [
        jnp.concatenate([r_ref[o * tiles + t] for t in range(tiles)], axis=1)
        for o in range(sensors // ROWS)
    ]
    misfit = jnp.concatenate(rows, axis=0)
    res_ref[...] = misfit[:, :steps]
    ys_ref[...] = product(misfit, high_ref, low_ref, slice(0, 2 * pad))
    xs_ref[...] = jnp.zeros_like(xs_ref)

    def column(c, carry):
        if sems is not None:
            column_copy(c, k_any, k_ref, sems).wait()
        for start, width in lane_blocks(freqs):
            rr = [ys_ref[top : top + ROWS, start : start + width] for top in range(0, sensors, ROWS)]
            ri = [ys_ref[top : top + ROWS, pad + start : pad + start + width] for top in range(0, sensors, ROWS)]
            for d in range(dips):
                real = jnp.zeros((ROWS, width), F32)
                imag = jnp.zeros((ROWS, width), F32)
                for i in range(sensors // ROWS):
                    kr = k_ref[0, c, d, i * ROWS : (i + 1) * ROWS, start : start + width]
                    ki = k_ref[1, c, d, i * ROWS : (i + 1) * ROWS, start : start + width]
                    real = real + (kr * rr[i] + ki * ri[i])
                    imag = imag + (kr * ri[i] - ki * rr[i])
                xs_ref[c, d : d + 1, start : start + width] = jnp.sum(real, axis=0, keepdims=True)
                xs_ref[c, d : d + 1, pad + start : pad + start + width] = jnp.sum(imag, axis=0, keepdims=True)
        return carry

    lax.fori_loop(0, cols, column, 0)
    spectra = xs_ref[...].reshape(cols * dips, 2 * pad)
    series = to_series(spectra[:, :pad], spectra[:, pad:], high_ref, low_ref, steps)
    even = lax.axis_index("param") % 2 == 0
    inner, outer = inner_ref[...], outer_ref[...]
    mine = lax.broadcasted_iota(jnp.int32, inner.shape, 0) == lax.axis_index("sensor")
    below = jnp.where(mine, jnp.where(even, outer, inner), 0.0)
    above = jnp.where(mine, jnp.where(even, inner, outer), 0.0)
    inside = jnp.zeros(((cols - 2) * dips, pad), F32)
    series -= LAMBDA_REG * jnp.concatenate([below, inside, above], axis=0)
    for j, tile in enumerate(packed(series, cols, steps)):
        for i in range(out_ref.shape[0]):
            out_ref[i, j] = tile


def first_adjoint_kernel(
    steps, r_ref, inner_ref, outer_ref, k_any, high_ref, low_ref, out_ref, res_ref, k_ref, xs_ref, ys_ref, sems
):
    adjoint_kernel(
        steps, r_ref, inner_ref, outer_ref, k_ref, high_ref, low_ref, out_ref, res_ref, xs_ref, ys_ref, k_any, sems
    )


def gradient_kernel(
    steps, parts_ref, s_ref, k_ref, high_ref, low_ref, out_ref, g_ref, xs_ref, ys_ref
):
    cols, dips = k_ref.shape[1:3]
    field = s_ref[...]
    count = cols * dips
    edge = jnp.zeros((dips, field.shape[1]), F32)
    earlier = jnp.concatenate([edge, field[: count - dips]], axis=0)
    later = jnp.concatenate([field[dips:], edge], axis=0)
    dip = lax.broadcasted_iota(jnp.int32, field.shape, 0) % dips
    upper = jnp.where(dip == 0, 0.0, pltpu.roll(field, 1, 0))
    lower = jnp.where(dip == dips - 1, 0.0, pltpu.roll(field, count - 1, 0))
    smooth = 4.0 * field - (earlier + later) - lower - upper
    summed = jnp.sum(parts_ref[...], axis=0)
    back = unpacked([summed[j] for j in range(summed.shape[0])], cols, steps)
    gradient = back + LAMBDA_REG * smooth
    g_ref[...] = gradient
    forward_map(gradient, None, high_ref, low_ref, out_ref, xs_ref, ys_ref, k_ref, None, steps)


def squares_kernel(params, groups, parts_ref, g_ref, out_ref):
    image = jnp.sum(parts_ref[...], axis=0)
    gradient = g_ref[...]
    image_sq = jnp.sum(image * image, keepdims=True)
    grad_sq = jnp.sum(gradient * gradient, keepdims=True) * (1.0 / groups)
    lane = lax.broadcasted_iota(jnp.int32, (1, LANES), 1)
    both = jnp.where(lane < LANES // 4, image_sq, grad_sq)
    out_ref[...] = jnp.broadcast_to(both[None], out_ref.shape)
    me, group = lax.axis_index("param"), lax.axis_index("sensor")
    points, pad = gradient.shape
    part = pad // groups

    def send(target, edge):
        tile = jnp.zeros((ROWS, LANES), F32)
        for t in range(pad // LANES):
            tile += jnp.where(group // 2 == t, edge[:, t * LANES : (t + 1) * LANES], 0.0)
        tile = jnp.where(group % 2 == 1, tile, pltpu.roll(tile, part, 1))
        out_ref[target] = jnp.where(lane < part, both, tile)

    @pl.when(me > 0)
    def _():
        send(me - 1, gradient[:ROWS])

    @pl.when(me < params - 1)
    def _():
        send(me + 1, gradient[points - ROWS :])


def shape(*dims):
    return jax.ShapeDtypeStruct(dims, F32)


def call(kernel, out_shape, scratch=(), outside=(), inputs=0):
    specs = [pl.BlockSpec(memory_space=pltpu.HBM if i in outside else pltpu.VMEM) for i in range(inputs)]
    return pl.pallas_call(
        kernel,
        out_shape=out_shape,
        scratch_shapes=[pltpu.VMEM(dims, F32) if isinstance(dims, tuple) else dims for dims in scratch],
        compiler_params=pltpu.CompilerParams(vmem_limit_bytes=VMEM_LIMIT),
        **({"in_specs": specs} if inputs else {}),
    )


def body(kernel_spec, observed, initial):
    _, cols, dips, sensors, freqs = kernel_spec.shape
    steps = observed.shape[1]
    points = cols * dips
    pad = -(-freqs // LANES) * LANES
    tiles = pad // LANES
    params = lax.axis_size("param")
    groups = lax.axis_size("sensor")
    assert params == sensors // ROWS * tiles and dips == ROWS
    assert cols * (steps % LANES) <= LANES and groups == dips and groups * LANES == 2 * pad
    high, low = (jnp.asarray(part) for part in dft_table(steps, freqs, pad))
    tiled = shape(params, ROWS, LANES)
    field = shape(points, pad)
    work = [(cols, dips, 2 * pad), (sensors, 2 * pad), kernel_spec.shape, pltpu.SemaphoreType.DMA((cols,))]
    swap = functools.partial(lax.all_to_all, split_axis=0, concat_axis=0)
    stay = functools.partial(pltpu.with_memory_space_constraint, memory_space=pltpu.HBM)
    spec = stay(kernel_spec)
    pairs = [(i, i ^ 1) for i in range(params)]
    others = [(i, i + 1 if i % 2 else i - 1) for i in range(1, params - 1)]
    edge = shape(dips, pad)
    map_work = work[:2]

    count = cols * (steps // LANES) + 1
    back = (shape(groups, count, ROWS, LANES), shape(sensors, steps))
    table = jax.ShapeDtypeStruct(high.shape, BF16)
    for iteration in range(ITERS):
        if iteration == 0:
            parts, sources, inner, outer, high, low = call(
                functools.partial(first_kernel, steps),
                (tiled, field, edge, edge, table, table),
                work + [pltpu.VMEM(initial.shape, F32), pltpu.SemaphoreType.DMA((3,))],
                outside=(0, 1, 2, 3),
                inputs=4,
            )(stay(initial), spec, stay(high), stay(low))
            inner, outer = lax.ppermute(inner, "param", pairs), lax.ppermute(outer, "param", others)
            parts, inner, outer = lax.optimization_barrier((swap(parts, "param"), inner, outer))
        else:
            parts, sources, inner, outer = call(
                functools.partial(step_kernel, steps, params), (tiled, field, edge, edge), map_work
            )(sources, gradient, sums, inner, outer, held, high, low)
            parts = swap(parts, "param")
        misfit = swap(call(misfit_kernel, tiled, [(ROWS, pad)])(parts, observed), "param")
        if iteration == 0:
            partial, residual, held = call(
                functools.partial(first_adjoint_kernel, steps),
                back + (shape(*kernel_spec.shape),),
                map_work + work[3:],
                outside=(3,),
                inputs=6,
            )(misfit, inner, outer, spec, high, low)
        else:
            partial, residual = call(functools.partial(adjoint_kernel, steps), back, map_work)(
                misfit, inner, outer, held, high, low
            )
        image, gradient = call(functools.partial(gradient_kernel, steps), (tiled, field), map_work)(
            swap(partial, "sensor"), sources, held, high, low
        )
        squares = call(functools.partial(squares_kernel, params, groups), shape(params, groups, LANES))(
            swap(image, "param"), gradient
        )
        sums = swap(squares.reshape(params * groups, 1, LANES), ("param", "sensor"))
        sums = sums.reshape(params, groups, LANES)
    sources = call(last_kernel, shape(cols, dips, steps))(sources, gradient, sums)
    return (sources, residual)


def solution(mesh):
    placed = (P(None, "param", None, "sensor", None), P("sensor", None), P("param", None, None))
    return jax.shard_map(
        body,
        mesh=mesh,
        in_specs=placed,
        out_specs=(P("param", None, None), P("sensor", None)),
        check_vma=False,
    )
```

```python
import functools
import math

import jax
import jax.numpy as jnp
import numpy as np
from jax import lax
from jax.experimental import pallas as pl
from jax.experimental.pallas import tpu as pltpu
from jax.sharding import PartitionSpec as P


ITERS = 2
LAMBDA_REG = 0.5
TINY_TERM = 1e-06
LANES = 128
ROWS = 8
F32 = jnp.float32
BF16 = jnp.bfloat16
VMEM_LIMIT = 20 * 1024 * 1024


def dft_table(steps, freqs, pad):
    index = np.arange(pad, dtype=np.int64)
    phase = (index[:, None] * index[None, :]) % (2 * steps)
    angle = phase * (math.pi / steps)
    inside = (index[:, None] < freqs) & (index[None, :] < freqs)
    whole = np.concatenate(
        [np.where(inside, np.cos(angle), 0.0), np.where(inside, -np.sin(angle), 0.0)], axis=1
    )
    high = whole.astype(np.float32).astype(BF16)
    low = (whole - high.astype(np.float64)).astype(np.float32).astype(BF16)
    return high, low


def product(x, high_ref, low_ref, columns):
    rows = x.shape[0]
    high = x.astype(BF16).astype(F32)
    terms = jnp.concatenate([high, x - high], axis=0).astype(BF16)
    dot = functools.partial(jnp.dot, preferred_element_type=F32)
    main = dot(terms, high_ref[:, columns])
    return main[:rows] + main[rows:] + dot(high.astype(BF16), low_ref[:, columns])


def to_series(real_part, imag_part, high_ref, low_ref, steps):
    pad = real_part.shape[1]
    column = lax.broadcasted_iota(jnp.int32, (1, pad), 1)
    weight = jnp.where((column == 0) | (column == steps), 1.0, 2.0) / (2.0 * steps)
    out = product(real_part * weight, high_ref, low_ref, slice(0, pad))
    out += product(imag_part * weight, high_ref, low_ref, slice(pad, 2 * pad))
    return jnp.where(column < steps, out, 0.0)


def lane_blocks(freqs):
    return [(start, min(LANES, freqs - start)) for start in range(0, freqs, LANES)]


def column_copy(c, k_any, k_ref, sems):
    return pltpu.make_async_copy(k_any.at[:, c], k_ref.at[:, c], sems.at[c])


def start_columns(k_any, k_ref, sems):
    for c in range(k_ref.shape[1] if sems is not None else 0):
        column_copy(c, k_any, k_ref, sems).start()


def forward_map(field, k_any, high_ref, low_ref, out_ref, xs_ref, ys_ref, k_ref, sems, steps):
    _, cols, dips, sensors, freqs = k_ref.shape
    pad = field.shape[1]
    xs_ref[...] = product(field, high_ref, low_ref, slice(0, 2 * pad)).reshape(cols, dips, 2 * pad)
    ys_ref[...] = jnp.zeros_like(ys_ref)
    height = min(8, sensors)

    def column(c, carry):
        if sems is not None:
            column_copy(c, k_any, k_ref, sems).wait()
        for start, width in lane_blocks(freqs):
            for top in range(0, sensors, height):
                rows = slice(top, top + height)
                real = ys_ref[rows, start : start + width]
                imag = ys_ref[rows, pad + start : pad + start + width]
                for d in range(dips):
                    kr = k_ref[0, c, d, rows, start : start + width]
                    ki = k_ref[1, c, d, rows, start : start + width]
                    xr = xs_ref[c, d : d + 1, start : start + width]
                    xi = xs_ref[c, d : d + 1, pad + start : pad + start + width]
                    real = real + (kr * xr - ki * xi)
                    imag = imag + (kr * xi + ki * xr)
                ys_ref[rows, start : start + width] = real
                ys_ref[rows, pad + start : pad + start + width] = imag
        return carry

    lax.fori_loop(0, cols, column, 0)
    series = to_series(ys_ref[:, :pad], ys_ref[:, pad:], high_ref, low_ref, steps)
    tiles = pad // LANES
    for o in range(sensors // ROWS):
        for t in range(tiles):
            out_ref[o * tiles + t] = series[o * ROWS : (o + 1) * ROWS, t * LANES : (t + 1) * LANES]


def store_edges(field, dips, inner_ref, outer_ref):
    even = lax.axis_index("param") % 2 == 0
    first, last = field[:dips], field[field.shape[0] - dips :]
    inner_ref[...] = jnp.where(even, last, first)
    outer_ref[...] = jnp.where(even, first, last)


def first_kernel(
    steps,
    s_any,
    k_any,
    high_any,
    low_any,
    out_ref,
    padded_ref,
    inner_ref,
    outer_ref,
    high_ref,
    low_ref,
    k_ref,
    xs_ref,
    ys_ref,
    sems,
    s_ref,
    table_sems,
):
    tables = [
        pltpu.make_async_copy(high_any, high_ref, table_sems.at[0]),
        pltpu.make_async_copy(low_any, low_ref, table_sems.at[1]),
    ]
    initial = pltpu.make_async_copy(s_any, s_ref, table_sems.at[2])
    initial.start()
    for copy in tables:
        copy.start()
    start_columns(k_any, k_ref, sems)
    cols, dips, _ = s_ref.shape
    padded_ref[...] = jnp.zeros_like(padded_ref)
    initial.wait()
    for c in range(cols):
        padded_ref[c * dips : (c + 1) * dips, :steps] = s_ref[c]
    store_edges(padded_ref[...], dips, inner_ref, outer_ref)
    for copy in tables:
        copy.wait()
    forward_map(padded_ref[...], k_any, high_ref, low_ref, out_ref, xs_ref, ys_ref, k_ref, sems, steps)


def step_size(sums_ref):
    sums = jnp.sum(jnp.sum(sums_ref[...], axis=0), axis=0, keepdims=True)
    image_sq = sums[:, :1]
    grad_sq = sums[:, LANES // 4 : LANES // 4 + 1]
    return grad_sq / (image_sq + 8.0 * LAMBDA_REG * grad_sq + TINY_TERM)


def stepped(field, gradient, alpha):
    return jnp.maximum(field - alpha * gradient, 0.0)


def gathered_row(sums_ref, neighbour, exists):
    lane = lax.broadcasted_iota(jnp.int32, (1, LANES), 1)
    came = sums_ref[jnp.where(exists, neighbour, 0)]
    turned = pltpu.roll(came, LANES // 2, 1)
    tiles = [
        jnp.where(lane < LANES // 2, turned[i : i + 1], came[i + 1 : i + 2]) for i in range(0, came.shape[0], 2)
    ]
    return jnp.where(exists, jnp.concatenate(tiles, axis=1), 0.0)


def step_kernel(
    steps,
    params,
    s_ref,
    g_ref,
    sums_ref,
    inner_ref,
    outer_ref,
    k_ref,
    high_ref,
    low_ref,
    out_ref,
    new_ref,
    new_inner_ref,
    new_outer_ref,
    xs_ref,
    ys_ref,
):
    me = lax.axis_index("param")
    even = me % 2 == 0
    alpha = step_size(sums_ref)
    new = stepped(s_ref[...], g_ref[...], alpha)
    new_ref[...] = new
    below = gathered_row(sums_ref, me - 1, me > 0)
    above = gathered_row(sums_ref, me + 1, me < params - 1)
    new_inner_ref[...] = stepped(inner_ref[...], jnp.where(even, above, below), alpha)
    new_outer_ref[...] = stepped(outer_ref[...], jnp.where(even, below, above), alpha)
    forward_map(new, None, high_ref, low_ref, out_ref, xs_ref, ys_ref, k_ref, None, steps)


def last_kernel(s_ref, g_ref, sums_ref, out_ref):
    new = stepped(s_ref[...], g_ref[...], step_size(sums_ref))
    cols, dips, steps = out_ref.shape
    for c in range(cols):
        out_ref[c] = new[c * dips : (c + 1) * dips, :steps]


def misfit_kernel(parts_ref, observed_ref, out_ref, padded_ref):
    steps = observed_ref.shape[1]
    tiles = padded_ref.shape[1] // LANES
    me = lax.axis_index("param")
    padded_ref[...] = jnp.zeros_like(padded_ref)
    padded_ref[:, :steps] = observed_ref[pl.ds(pl.multiple_of(me // tiles * ROWS, ROWS), ROWS), :]
    misfit = jnp.sum(parts_ref[...], axis=0)
    for t in range(tiles):
        misfit -= jnp.where(me % tiles == t, padded_ref[:, t * LANES : (t + 1) * LANES], 0.0)
    out_ref[...] = jnp.broadcast_to(misfit[None], out_ref.shape)


def packed(series, cols, steps):
    whole = steps // LANES
    width = steps - whole * LANES
    tiles = []
    tail = None
    for c in range(cols):
        rows = series[c * ROWS : (c + 1) * ROWS]
        tiles += [rows[:, t * LANES : (t + 1) * LANES] for t in range(whole)]
        end = rows[:, whole * LANES :]
        tail = end if tail is None else tail + pltpu.roll(end, c * width, 1)
    return tiles + [tail]


def unpacked(tiles, cols, steps):
    whole = steps // LANES
    width = steps - whole * LANES
    lane = lax.broadcasted_iota(jnp.int32, (ROWS, LANES), 1)
    tail = tiles[cols * whole]
    rows = []
    for c in range(cols):
        end = pltpu.roll(tail, LANES - c * width, 1) if c else tail
        parts = [tiles[c * whole + t] for t in range(whole)] + [jnp.where(lane < width, end, 0.0)]
        rows.append(jnp.concatenate(parts, axis=1))
    return jnp.concatenate(rows, axis=0)


def adjoint_kernel(
    steps, r_ref, inner_ref, outer_ref, k_ref, high_ref, low_ref, out_ref, res_ref, xs_ref, ys_ref
):
    _, cols, dips, sensors, freqs = k_ref.shape
    pad = xs_ref.shape[2] // 2
    tiles = pad // LANES
    rows = [
        jnp.concatenate([r_ref[o * tiles + t] for t in range(tiles)], axis=1)
        for o in range(sensors // ROWS)
    ]
    misfit = jnp.concatenate(rows, axis=0)
    res_ref[...] = misfit[:, :steps]
    ys_ref[...] = product(misfit, high_ref, low_ref, slice(0, 2 * pad))
    xs_ref[...] = jnp.zeros_like(xs_ref)

    def column(c, carry):
        for start, width in lane_blocks(freqs):
            rr = [ys_ref[top : top + ROWS, start : start + width] for top in range(0, sensors, ROWS)]
            ri = [ys_ref[top : top + ROWS, pad + start : pad + start + width] for top in range(0, sensors, ROWS)]
            for d in range(dips):
                real = jnp.zeros((ROWS, width), F32)
                imag = jnp.zeros((ROWS, width), F32)
                for i in range(sensors // ROWS):
                    kr = k_ref[0, c, d, i * ROWS : (i + 1) * ROWS, start : start + width]
                    ki = k_ref[1, c, d, i * ROWS : (i + 1) * ROWS, start : start + width]
                    real = real + (kr * rr[i] + ki * ri[i])
                    imag = imag + (kr * ri[i] - ki * rr[i])
                xs_ref[c, d : d + 1, start : start + width] = jnp.sum(real, axis=0, keepdims=True)
                xs_ref[c, d : d + 1, pad + start : pad + start + width] = jnp.sum(imag, axis=0, keepdims=True)
        return carry

    lax.fori_loop(0, cols, column, 0)
    spectra = xs_ref[...].reshape(cols * dips, 2 * pad)
    series = to_series(spectra[:, :pad], spectra[:, pad:], high_ref, low_ref, steps)
    even = lax.axis_index("param") % 2 == 0
    inner, outer = inner_ref[...], outer_ref[...]
    mine = lax.broadcasted_iota(jnp.int32, inner.shape, 0) == lax.axis_index("sensor")
    below = jnp.where(mine, jnp.where(even, outer, inner), 0.0)
    above = jnp.where(mine, jnp.where(even, inner, outer), 0.0)
    inside = jnp.zeros(((cols - 2) * dips, pad), F32)
    series -= LAMBDA_REG * jnp.concatenate([below, inside, above], axis=0)
    for j, tile in enumerate(packed(series, cols, steps)):
        for i in range(out_ref.shape[0]):
            out_ref[i, j] = tile


def gradient_kernel(
    steps, parts_ref, s_ref, k_ref, high_ref, low_ref, out_ref, g_ref, xs_ref, ys_ref
):
    cols, dips = k_ref.shape[1:3]
    field = s_ref[...]
    count = cols * dips
    edge = jnp.zeros((dips, field.shape[1]), F32)
    earlier = jnp.concatenate([edge, field[: count - dips]], axis=0)
    later = jnp.concatenate([field[dips:], edge], axis=0)
    dip = lax.broadcasted_iota(jnp.int32, field.shape, 0) % dips
    upper = jnp.where(dip == 0, 0.0, pltpu.roll(field, 1, 0))
    lower = jnp.where(dip == dips - 1, 0.0, pltpu.roll(field, count - 1, 0))
    smooth = 4.0 * field - (earlier + later) - lower - upper
    summed = jnp.sum(parts_ref[...], axis=0)
    back = unpacked([summed[j] for j in range(summed.shape[0])], cols, steps)
    gradient = back + LAMBDA_REG * smooth
    g_ref[...] = gradient
    forward_map(gradient, None, high_ref, low_ref, out_ref, xs_ref, ys_ref, k_ref, None, steps)


def squares_kernel(params, groups, parts_ref, g_ref, out_ref):
    image = jnp.sum(parts_ref[...], axis=0)
    gradient = g_ref[...]
    image_sq = jnp.sum(image * image, keepdims=True)
    grad_sq = jnp.sum(gradient * gradient, keepdims=True) * (1.0 / groups)
    lane = lax.broadcasted_iota(jnp.int32, (1, LANES), 1)
    both = jnp.where(lane < LANES // 4, image_sq, grad_sq)
    out_ref[...] = jnp.broadcast_to(both[None], out_ref.shape)
    me, group = lax.axis_index("param"), lax.axis_index("sensor")
    points, pad = gradient.shape
    part = pad // groups

    def send(target, edge):
        tile = jnp.zeros((ROWS, LANES), F32)
        for t in range(pad // LANES):
            tile += jnp.where(group // 2 == t, edge[:, t * LANES : (t + 1) * LANES], 0.0)
        tile = jnp.where(group % 2 == 1, tile, pltpu.roll(tile, part, 1))
        out_ref[target] = jnp.where(lane < part, both, tile)

    @pl.when(me > 0)
    def _():
        send(me - 1, gradient[:ROWS])

    @pl.when(me < params - 1)
    def _():
        send(me + 1, gradient[points - ROWS :])


def shape(*dims):
    return jax.ShapeDtypeStruct(dims, F32)


def call(kernel, out_shape, scratch=(), outside=(), inputs=0):
    specs = [pl.BlockSpec(memory_space=pltpu.HBM if i in outside else pltpu.VMEM) for i in range(inputs)]
    return pl.pallas_call(
        kernel,
        out_shape=out_shape,
        scratch_shapes=[pltpu.VMEM(dims, F32) if isinstance(dims, tuple) else dims for dims in scratch],
        compiler_params=pltpu.CompilerParams(vmem_limit_bytes=VMEM_LIMIT),
        **({"in_specs": specs} if inputs else {}),
    )


def body(kernel_spec, observed, initial):
    _, cols, dips, sensors, freqs = kernel_spec.shape
    steps = observed.shape[1]
    points = cols * dips
    pad = -(-freqs // LANES) * LANES
    tiles = pad // LANES
    params = lax.axis_size("param")
    groups = lax.axis_size("sensor")
    assert params == sensors // ROWS * tiles and dips == ROWS
    assert cols * (steps % LANES) <= LANES and groups == dips and groups * LANES == 2 * pad
    high, low = (jnp.asarray(part) for part in dft_table(steps, freqs, pad))
    tiled = shape(params, ROWS, LANES)
    field = shape(points, pad)
    work = [(cols, dips, 2 * pad), (sensors, 2 * pad), pltpu.SemaphoreType.DMA((cols,))]
    swap = functools.partial(lax.all_to_all, split_axis=0, concat_axis=0)
    stay = functools.partial(pltpu.with_memory_space_constraint, memory_space=pltpu.HBM)
    spec = stay(kernel_spec)
    pairs = [(i, i ^ 1) for i in range(params)]
    others = [(i, i + 1 if i % 2 else i - 1) for i in range(1, params - 1)]
    edge = shape(dips, pad)
    map_work = work[:2]

    count = cols * (steps // LANES) + 1
    back = (shape(groups, count, ROWS, LANES), shape(sensors, steps))
    table = jax.ShapeDtypeStruct(high.shape, BF16)
    for iteration in range(ITERS):
        if iteration == 0:
            parts, sources, inner, outer, high, low, held = call(
                functools.partial(first_kernel, steps),
                (tiled, field, edge, edge, table, table, shape(*kernel_spec.shape)),
                work + [pltpu.VMEM(initial.shape, F32), pltpu.SemaphoreType.DMA((3,))],
                outside=(0, 1, 2, 3),
                inputs=4,
            )(stay(initial), spec, stay(high), stay(low))
            inner = lax.ppermute(inner, "param", pairs)
            outer = lax.ppermute(outer, "param", others)
            parts = swap(parts, "param")
        else:
            parts, sources, inner, outer = call(
                functools.partial(step_kernel, steps, params), (tiled, field, edge, edge), map_work
            )(sources, gradient, sums, inner, outer, held, high, low)
            parts = swap(parts, "param")
        misfit = call(misfit_kernel, tiled, [(ROWS, pad)])(parts, observed)
        if iteration == 0:
            misfit, inner, outer = lax.optimization_barrier((misfit, inner, outer))
        misfit = swap(misfit, "param")
        partial, residual = call(functools.partial(adjoint_kernel, steps), back, map_work)(
            misfit, inner, outer, held, high, low
        )
        image, gradient = call(functools.partial(gradient_kernel, steps), (tiled, field), map_work)(
            swap(partial, "sensor"), sources, held, high, low
        )
        squares = call(functools.partial(squares_kernel, params, groups), shape(params, groups, LANES))(
            swap(image, "param"), gradient
        )
        sums = swap(squares.reshape(params * groups, 1, LANES), ("param", "sensor"))
        sums = sums.reshape(params, groups, LANES)
    sources = call(last_kernel, shape(cols, dips, steps))(sources, gradient, sums)
    return (sources, residual)


def solution(mesh):
    placed = (P(None, "param", None, "sensor", None), P("sensor", None), P("param", None, None))
    return jax.shard_map(
        body,
        mesh=mesh,
        in_specs=placed,
        out_specs=(P("param", None, None), P("sensor", None)),
        check_vma=False,
    )
```
